512 devices in a mesh: box: 64 (over z_hi, y, core), src: 8 (over z_lo, x).
Axes of the slice: x: 4, y: 8, z: 8 (z_hi: 4, z_lo: 2; z = z_hi * 2 + z_lo), core: 2. Of those that a mesh axis runs over, the one named last changes fastest.
Arguments:
- incident: bfloat16 [512, 1024, 256], P('box', 'src'), may hold values from -6 to 6
- reflectivity: float32 [512, 128], P('box'), may hold values from 0.5 to 2
- w_self: bfloat16 [3, 512, 2, 128, 128], P(None, 'box'), may hold values from -0.25 to 0.25
- w_cross: bfloat16 [3, 512, 2, 128, 128], P(None, 'box'), may hold values from -0.25 to 0.25
- receivers: int32 [512], P('box'), may hold values from 0 to 511, as said below
- observed: bfloat16 [512, 1024, 256], P('box', 'src'), may hold values from -6 to 6
- group_of: int32 [1024], P('src'), may hold values from 0 to 15
- deltas: float32 [16], replicated, may hold values from 0.5 to 4
Outputs:
- image_grad: float32 [512, 128], P('box', 'src')
The draws below stay inside these ranges and needn't reach their ends.
Inputs may be any that keep to these rules, and one draw needn't show every extreme that they name: `receivers`: trace t lies in box block t // 8, that is between (8 * (t // 8)) and (8 * (t // 8) + 7).
All inputs are finite; a program needn't handle non-finite values.
Results may differ from the reference program's by a relative error of at most 0.001.
Values may be sent and summed in bfloat16 or wider, within the bound.
No kernel may reach another device: no remote copies, remote signals or barrier semaphores. Data moves between devices by JAX's collectives and lax.ppermute only.
A program may use at most 64 MiB of HBM per device.

```python
import math
import jax
import jax.numpy as jnp
from jax import lax

NODES = 128
BOX_DEV = 8
SECTIONS = 3
TRACES = 8
NGROUPS = 16
NB = 512
SOURCES = 1024
NT = 512
N_BOX = 64


def draw_receivers(key, part):
    positions = jnp.arange(NT, dtype=jnp.int32)
    block_base = positions // TRACES * BOX_DEV
    offsets = jax.random.randint(key, (NT,), 0, BOX_DEV, dtype=jnp.int32)
    trace_slot = positions % TRACES
    offsets = jnp.where(trace_slot == 0, BOX_DEV - 1, jnp.where(trace_slot == 1, 0, offsets))
    return (block_base + offsets).astype(jnp.int32)


def with_ends(drawn, rng, smallest, largest):
    extent = drawn.shape
    spot = [jax.random.randint(jax.random.fold_in(rng, axis), (), 0, extent[axis]) for axis in range(len(extent))]
    drawn = drawn.at[tuple(spot)].set(smallest)
    longest = extent.index(max(extent))
    spot[longest] = (spot[longest] + 1) % extent[longest]
    return drawn.at[tuple(spot)].set(largest)


def block_levels(own_key, extent, cuts, low, largest):
    gain = 1.0
    for dim, blocks in cuts:
        steps = jax.random.uniform(jax.random.fold_in(jax.random.fold_in(own_key, 6), dim), (blocks,), jnp.float32, low / len(cuts), largest / len(cuts))
        gain = gain * jnp.repeat(jnp.exp(steps), extent[dim] // blocks).reshape((-1,) + (1,) * (len(extent) - 1 - dim))
    return gain


def scatter_about(stream_key, extent, spread, most, pieces=(), held_as=jnp.bfloat16):
    result = spread * jax.random.normal(stream_key, extent, jnp.float32)
    if pieces:
        result = result * block_levels(stream_key, extent, pieces, -0.22, 0.18)
    return jnp.clip(result, -most, most).astype(held_as)


def setup_inputs(seed: int = 0) -> dict:
    key_list = jax.random.split(jax.random.key(seed), 9)
    return {
        "incident": scatter_about(key_list[0], (NB, SOURCES, 2 * NODES), 1.0, 6.0, ((0, 64), (1, 8))),
        "reflectivity": jnp.clip(jnp.exp(math.log(2.0) - 1.3862944 * jax.random.uniform(key_list[1], (NB, NODES), jnp.float32) ** block_levels(key_list[1], (NB, NODES), ((0, 64),), -0.2, 0.2)), 0.5, 2.0),
        "w_self": scatter_about(key_list[2], (SECTIONS, NB, 2, NODES, NODES), (4 * NODES) ** -0.5, 0.25, ((1, 64),)),
        "w_cross": scatter_about(key_list[3], (SECTIONS, NB, 2, NODES, NODES), (4 * NODES) ** -0.5, 0.25, ((1, 64),)),
        "receivers": draw_receivers(jax.random.fold_in(key_list[8], 71), 0),
        "observed": scatter_about(key_list[5], (NT, SOURCES, 2 * NODES), 1.0, 6.0, ((0, 64), (1, 8))),
        "group_of": with_ends(jax.random.randint(key_list[6], (SOURCES,), 0, NGROUPS), jax.random.fold_in(key_list[6], 1), 0, NGROUPS - 1).astype(jnp.int32),
        "deltas": jnp.clip(jnp.exp(jax.random.uniform(key_list[7], (NGROUPS,), jnp.float32, math.log(0.5), math.log(4.0))), 0.5, 4.0),
    }


def block_form(weights):
    real_part = weights[:, 0].astype(jnp.float32)
    imag_part = weights[:, 1].astype(jnp.float32)
    upper_rows = jnp.concatenate([real_part, imag_part], axis=2)
    lower_rows = jnp.concatenate([-imag_part, real_part], axis=2)
    return jnp.concatenate([upper_rows, lower_rows], axis=1)

def partner_of(values, swap_bit):
    blocks = values.reshape((N_BOX, BOX_DEV) + values.shape[1:])
    order = (jnp.arange(N_BOX, dtype=jnp.int32) ^ 1 << swap_bit).astype(jnp.int32)
    return blocks[order].reshape(values.shape)

def forward_apply(values, block):
    return jnp.einsum('bsi,bij->bsj', values.astype(jnp.float32), block)

def adjoint_apply(values, block):
    return jnp.einsum('bsj,bij->bsi', values.astype(jnp.float32), block)

def reference(incident, reflectivity, w_self, w_cross, receivers, observed, group_of, deltas):
    top_bit = N_BOX.bit_length() - 1
    doubled = jnp.concatenate([reflectivity, reflectivity], axis=1)
    wavefield = (doubled[:, None, :] * incident.astype(jnp.float32)).astype(jnp.bfloat16)
    for section_idx in range(SECTIONS):
        swap_bit = top_bit - 1 - section_idx
        partner_field = partner_of(wavefield, swap_bit)
        summed = forward_apply(wavefield, block_form(w_self[section_idx])) + forward_apply(partner_field, block_form(w_cross[section_idx]))
        wavefield = summed.astype(jnp.bfloat16)
    predicted = wavefield[receivers].astype(jnp.float32)
    residual = predicted - observed.astype(jnp.float32)
    magnitude = residual[..., :NODES] ** 2 + residual[..., NODES:] ** 2
    scale_src = deltas[group_of]
    damping = 1.0 / jnp.sqrt(1.0 + magnitude / scale_src[None, :, None] ** 2)
    adj_traces = (residual * jnp.concatenate([damping, damping], axis=2)).astype(jnp.bfloat16)
    adjoint_field = jax.ops.segment_sum(adj_traces.astype(jnp.float32), receivers, num_segments=NB).astype(jnp.bfloat16)
    for section_idx in reversed(range(SECTIONS)):
        swap_bit = top_bit - 1 - section_idx
        outgoing = adjoint_apply(adjoint_field, block_form(w_cross[section_idx])).astype(jnp.bfloat16)
        received = partner_of(outgoing, swap_bit)
        summed = adjoint_apply(adjoint_field, block_form(w_self[section_idx])) + received.astype(jnp.float32)
        adjoint_field = summed.astype(jnp.bfloat16)
    products = incident.astype(jnp.float32) * adjoint_field.astype(jnp.float32)
    return lax.optimization_barrier(jnp.sum(products[..., :NODES] + products[..., NODES:], axis=1))
```

```python
import jax
import jax.numpy as jnp
from jax import lax
from jax.sharding import PartitionSpec as P

CHUNKS = 2


def from_partner(x, axis, distance):
    return lax.ppermute(x, axis, [(i, i ^ 1 << distance) for i in range(lax.axis_size(axis))])


def block_form(weights):
    real_part = weights[:, 0]
    imag_part = weights[:, 1]
    upper_rows = jnp.concatenate([real_part, imag_part], axis=2)
    lower_rows = jnp.concatenate([-imag_part, real_part], axis=2)
    return jnp.concatenate([upper_rows, lower_rows], axis=1)


def forward_apply(values, block):
    return jnp.einsum("bsi,bij->bsj", values, block, preferred_element_type=jnp.float32)


def adjoint_apply(values, block):
    return jnp.einsum("bsj,bij->bsi", values, block, preferred_element_type=jnp.float32)


def image_terms(incident, adjoint):
    products = incident.astype(jnp.float32) * adjoint
    node_count = products.shape[2] // 2
    return jnp.sum(products[..., :node_count] + products[..., node_count:], axis=1)


def body(incident, reflectivity, w_self, w_cross, receivers, observed, group_of, deltas):
    box_count, source_count, width = incident.shape
    node_count = width // 2
    sections = w_self.shape[0]
    box_devices = lax.axis_size("box")
    src_devices = lax.axis_size("src")
    top_bit = box_devices.bit_length() - 1
    swap_bits = [top_bit - 1 - section for section in range(sections)]
    block_start = lax.axis_index("box") * box_count
    onehot = (
        (receivers - block_start)[:, None] == jnp.arange(box_count, dtype=jnp.int32)[None, :]
    ).astype(jnp.bfloat16)
    group_hits = (
        group_of[:, None] == jnp.arange(deltas.shape[0], dtype=jnp.int32)[None, :]
    ).astype(jnp.float32)
    scale_src = jnp.sum(group_hits * deltas[None, :], axis=1)
    step = source_count // CHUNKS
    spans = [slice(c * step, (c + 1) * step) for c in range(CHUNKS)]

    incidents = [incident[:, span] for span in spans]
    partner_incidents = [from_partner(x, "box", swap_bits[0]) for x in incidents]
    partner_reflectivity = from_partner(reflectivity, "box", swap_bits[0])
    self_blocks = [block_form(w_self[section]) for section in range(sections)]
    cross_blocks = [block_form(w_cross[section]) for section in range(sections)]

    def scaled(field, gains):
        doubled = jnp.concatenate([gains, gains], axis=1)
        return (doubled[:, None, :] * field.astype(jnp.float32)).astype(jnp.bfloat16)

    fields = [scaled(x, reflectivity) for x in incidents]
    partners = [scaled(x, partner_reflectivity) for x in partner_incidents]
    for section in range(sections):
        if section:
            partners = [from_partner(x, "box", swap_bits[section]) for x in fields]
        fields = [
            (
                forward_apply(x, self_blocks[section]) + forward_apply(p, cross_blocks[section])
            ).astype(jnp.bfloat16)
            for x, p in zip(fields, partners)
        ]
    adjoints = []
    for span, field in zip(spans, fields):
        predicted = jnp.einsum("kb,bsi->ksi", onehot, field, preferred_element_type=jnp.float32)
        residual = predicted - observed[:, span].astype(jnp.float32)
        magnitude = residual[..., :node_count] ** 2 + residual[..., node_count:] ** 2
        damping = 1.0 / jnp.sqrt(1.0 + magnitude / scale_src[None, span, None] ** 2)
        adj_traces = (residual * jnp.concatenate([damping, damping], axis=2)).astype(jnp.bfloat16)
        adjoints.append(
            jnp.einsum(
                "kb,ksi->bsi", onehot, adj_traces, preferred_element_type=jnp.float32
            ).astype(jnp.bfloat16)
        )
    for section in range(sections - 1, 0, -1):
        received = [
            from_partner(
                adjoint_apply(x, cross_blocks[section]).astype(jnp.bfloat16),
                "box",
                swap_bits[section],
            )
            for x in adjoints
        ]
        adjoints = [
            (adjoint_apply(x, self_blocks[section]) + r.astype(jnp.float32)).astype(jnp.bfloat16)
            for x, r in zip(adjoints, received)
        ]
    own = sum(
        image_terms(x, adjoint_apply(a, self_blocks[0])) for x, a in zip(incidents, adjoints)
    )
    other = sum(
        image_terms(x, adjoint_apply(a, cross_blocks[0]))
        for x, a in zip(partner_incidents, adjoints)
    )
    share = node_count // src_devices
    both = jnp.concatenate([own, other], axis=0)
    pieces = both.reshape(2 * box_count, src_devices, share).transpose(1, 0, 2)
    gathered = lax.all_to_all(pieces, "src", 0, 0)
    totals = jnp.sum(gathered, axis=0)
    return totals[:box_count] + from_partner(totals[box_count:], "box", swap_bits[0])


def solution(mesh):
    in_specs = (
        P("box", "src", None),
        P("box", None),
        P(None, "box", None, None, None),
        P(None, "box", None, None, None),
        P("box"),
        P("box", "src", None),
        P("src"),
        P(),
    )
    out_specs = P("box", "src")
    return jax.shard_map(body, mesh=mesh, in_specs=in_specs, out_specs=out_specs, check_vma=False)
```

```python
import jax
import jax.numpy as jnp
from jax import lax
from jax.sharding import PartitionSpec as P


CHUNKS = 2


def send(x, axis, flip):
    return lax.ppermute(x, axis, [(i, i ^ flip) for i in range(lax.axis_size(axis))])


def block_form(weights):
    real_part = weights[:, 0]
    imag_part = weights[:, 1]
    upper_rows = jnp.concatenate([real_part, imag_part], axis=2)
    lower_rows = jnp.concatenate([-imag_part, real_part], axis=2)
    return jnp.concatenate([upper_rows, lower_rows], axis=1)


def forward_apply(values, block):
    return jnp.einsum("bsi,bij->bsj", values, block, preferred_element_type=jnp.float32)


def adjoint_apply(values, block):
    return jnp.einsum("bsj,bij->bsi", values, block, preferred_element_type=jnp.float32)


def stage(field, partner, own, cross):
    return (forward_apply(field, own) + forward_apply(partner, cross)).astype(jnp.bfloat16)


def image_terms(incident, adjoint):
    products = incident.astype(jnp.float32) * adjoint
    node_count = products.shape[2] // 2
    return jnp.sum(products[..., :node_count] + products[..., node_count:], axis=1)


def scaled(field, gains):
    doubled = jnp.concatenate([gains, gains], axis=1)
    return (doubled[:, None, :] * field.astype(jnp.float32)).astype(jnp.bfloat16)


def split_gains(gains):
    high = lax.reduce_precision(gains, 8, 7)
    rest = gains - high
    middle = lax.reduce_precision(rest, 8, 7)
    low = rest - middle
    rows = jnp.stack(
        [
            jnp.concatenate([high, middle], axis=1),
            jnp.concatenate([low, jnp.zeros_like(low)], axis=1),
        ],
        axis=1,
    ).astype(jnp.bfloat16)
    return jnp.pad(rows, ((0, 0), (0, 6), (0, 0)))


def join_gains(rows):
    node_count = rows.shape[2] // 2
    rows = rows.astype(jnp.float32)
    return (rows[:, 0, :node_count] + rows[:, 0, node_count:]) + rows[:, 1, :node_count]


def trace_adjoint(field, onehot, observed, scale):
    predicted = jnp.einsum("kb,bsi->ksi", onehot, field, preferred_element_type=jnp.float32)
    residual = predicted - observed.astype(jnp.float32)
    node_count = residual.shape[2] // 2
    magnitude = residual[..., :node_count] ** 2 + residual[..., node_count:] ** 2
    damping = 1.0 / jnp.sqrt(1.0 + magnitude / scale[None, :, None] ** 2)
    adj_traces = (residual * jnp.concatenate([damping, damping], axis=2)).astype(jnp.bfloat16)
    return jnp.einsum("kb,ksi->bsi", onehot, adj_traces, preferred_element_type=jnp.float32).astype(
        jnp.bfloat16
    )


def both_weights(sent_self, sent_cross, odd, flip):
    first = send(jnp.where(odd, sent_cross, sent_self), "box", flip)
    second = send(first, "src", 1)
    return jnp.where(odd, second, first), jnp.where(odd, first, second)


def body(incident, reflectivity, w_self, w_cross, receivers, observed, group_of, deltas):
    box_count, source_count, width = incident.shape
    node_count = width // 2
    box_devices = lax.axis_size("box")
    src_devices = lax.axis_size("src")
    flip0, flip1, flip2 = box_devices // 2, box_devices // 4, box_devices // 8
    box_index = lax.axis_index("box")
    odd = lax.axis_index("src") % 2 == 1
    onehot = (
        (receivers - box_index * box_count)[:, None]
        == jnp.arange(box_count, dtype=jnp.int32)[None, :]
    ).astype(jnp.bfloat16)
    group_hits = (
        group_of[:, None] == jnp.arange(deltas.shape[0], dtype=jnp.int32)[None, :]
    ).astype(jnp.float32)
    scale_src = jnp.sum(group_hits * deltas[None, :], axis=1)
    step = source_count // CHUNKS
    spans = [slice(c * step, (c + 1) * step) for c in range(CHUNKS)]

    incidents = [incident[:, span] for span in spans]
    sent = list(incidents)
    sent[0] = jnp.concatenate([sent[0], split_gains(reflectivity)], axis=1)
    came = [send(x, "box", flip0) for x in sent]
    across_gains = join_gains(came[0][:, step:])
    across_incidents = [x[:, :step] for x in came]

    far_self2, far_cross2 = both_weights(w_self[2], w_cross[2], odd, flip2)
    tag = jnp.pad(onehot[:, None, :], ((0, 0), (0, 7), (0, width - box_count)))
    far_traces = send(jnp.concatenate([observed, tag], axis=1), "box", flip2)
    far_observed = far_traces[:, :source_count]
    far_onehot = far_traces[:, source_count, :box_count]

    self0, cross0 = block_form(w_self[0]), block_form(w_cross[0])
    fields = [
        stage(scaled(x, reflectivity), scaled(p, across_gains), self0, cross0)
        for x, p in zip(incidents, across_incidents)
    ]
    nears = [send(x, "box", flip1) for x in fields]
    weights_self, weights_cross, _ = lax.optimization_barrier((w_self[1], w_cross[1], fields))
    self1, cross1 = block_form(weights_self), block_form(weights_cross)
    fields = [stage(x, p, self1, cross1) for x, p in zip(fields, nears)]
    partners = [send(x, "box", flip2) for x in fields]
    weights_self, weights_cross, _ = lax.optimization_barrier((w_self[2], w_cross[2], fields))
    self2, cross2 = block_form(weights_self), block_form(weights_cross)
    far_self2, far_cross2 = block_form(far_self2), block_form(far_cross2)

    adjoints = []
    received = []
    for c, (span, field, partner) in enumerate(zip(spans, fields, partners)):
        if c:
            partner, _ = lax.optimization_barrier((partner, outgoing))
        top = stage(field, partner, self2, cross2)
        far_top = stage(partner, field, far_self2, far_cross2)
        own = trace_adjoint(top, onehot, observed[:, span], scale_src[span])
        far = trace_adjoint(far_top, far_onehot, far_observed[:, span], scale_src[span])
        adjoint = adjoint_apply(own, self2) + adjoint_apply(far, far_cross2)
        adjoints.append(adjoint.astype(jnp.bfloat16))
        outgoing = adjoint_apply(adjoints[-1], cross1).astype(jnp.bfloat16)
        received.append(send(outgoing, "box", flip1))
    adjoints = [
        (adjoint_apply(x, self1) + r.astype(jnp.float32)).astype(jnp.bfloat16)
        for x, r in zip(adjoints, received)
    ]
    own = across = 0.0
    for x, p, a in zip(incidents, across_incidents, adjoints):
        own += image_terms(x, adjoint_apply(a, self0))
        across += image_terms(p, adjoint_apply(a, cross0))

    share = node_count // src_devices
    upper = (box_index & flip0) != 0
    both = jnp.where(upper, jnp.stack([across, own]), jnp.stack([own, across]))
    pieces = both.reshape(2, box_count, src_devices, share).transpose(0, 2, 1, 3)
    pieces = pieces.reshape(2 * src_devices, box_count, share)
    groups = [
        [b * src_devices + s for b in (g, g + flip0) for s in range(src_devices)]
        for g in range(flip0)
    ]
    gathered = lax.all_to_all(pieces, ("box", "src"), 0, 0, axis_index_groups=groups)
    return jnp.sum(gathered, axis=0)


def solution(mesh):
    in_specs = (
        P("box", "src", None),
        P("box", None),
        P(None, "box", None, None, None),
        P(None, "box", None, None, None),
        P("box"),
        P("box", "src", None),
        P("src"),
        P(),
    )
    out_specs = P("box", "src")

    return jax.shard_map(body, mesh=mesh, in_specs=in_specs, out_specs=out_specs, check_vma=False)
```

```python
import jax
import jax.numpy as jnp
from jax import lax
from jax.sharding import PartitionSpec as P


CHUNKS = (64, 64)


def send(x, axis, flip):
    return lax.ppermute(x, axis, [(i, i ^ flip) for i in range(lax.axis_size(axis))])


def join_parts(real_part, imag_part):
    upper_rows = jnp.concatenate([real_part, imag_part], axis=2)
    lower_rows = jnp.concatenate([-imag_part, real_part], axis=2)
    return jnp.concatenate([upper_rows, lower_rows], axis=1)


def block_form(weights):
    return join_parts(weights[:, 0], weights[:, 1])


def forward_apply(values, block):
    return jnp.einsum("bsi,bij->bsj", values, block, preferred_element_type=jnp.float32)


def adjoint_apply(values, block):
    return jnp.einsum("bsj,bij->bsi", values, block, preferred_element_type=jnp.float32)


def stage(field, partner, own, cross):
    kept = forward_apply(field, own)
    return (kept + forward_apply(partner, cross)).astype(jnp.bfloat16)


def image_terms(incident, adjoint):
    products = incident.astype(jnp.float32) * adjoint
    node_count = products.shape[2] // 2
    return jnp.sum(products[..., :node_count] + products[..., node_count:], axis=1)


def scaled(field, gains):
    doubled = jnp.concatenate([gains, gains], axis=1)
    return (doubled[:, None, :] * field.astype(jnp.float32)).astype(jnp.bfloat16)


def split_gains(gains):
    high = lax.reduce_precision(gains, 8, 7)
    rest = gains - high
    middle = lax.reduce_precision(rest, 8, 7)
    low = rest - middle
    rows = jnp.stack(
        [
            jnp.concatenate([high, middle], axis=1),
            jnp.concatenate([low, jnp.zeros_like(low)], axis=1),
        ],
        axis=1,
    ).astype(jnp.bfloat16)
    return jnp.pad(rows, ((0, 0), (0, 6), (0, 0)))


def join_gains(rows):
    node_count = rows.shape[2] // 2
    rows = rows.astype(jnp.float32)
    return (rows[:, 0, :node_count] + rows[:, 0, node_count:]) + rows[:, 1, :node_count]


def trace_adjoint(field, onehot, observed, scale):
    predicted = jnp.einsum("kb,bsi->ksi", onehot, field, preferred_element_type=jnp.float32)
    residual = predicted - observed.astype(jnp.float32)
    node_count = residual.shape[2] // 2
    magnitude = residual[..., :node_count] ** 2 + residual[..., node_count:] ** 2
    damping = 1.0 / jnp.sqrt(1.0 + magnitude / scale[None, :, None] ** 2)
    adj_traces = (residual * jnp.concatenate([damping, damping], axis=2)).astype(jnp.bfloat16)
    return jnp.einsum("kb,ksi->bsi", onehot, adj_traces, preferred_element_type=jnp.float32).astype(
        jnp.bfloat16
    )


def pick(parts, index):
    low, high = (index & 1) != 0, (index & 2) != 0
    return jnp.where(high, jnp.where(low, parts[3], parts[2]), jnp.where(low, parts[1], parts[0]))


def body(incident, reflectivity, w_self, w_cross, receivers, observed, group_of, deltas):
    box_count, source_count, width = incident.shape
    node_count = width // 2
    box_devices = lax.axis_size("box")
    src_devices = lax.axis_size("src")
    flip0, flip1, flip2 = box_devices // 2, box_devices // 4, box_devices // 8
    box_index = lax.axis_index("box")
    quarter = lax.axis_index("src") % 4
    onehot = (
        (receivers - box_index * box_count)[:, None]
        == jnp.arange(box_count, dtype=jnp.int32)[None, :]
    ).astype(jnp.bfloat16)
    group_hits = (
        group_of[:, None] == jnp.arange(deltas.shape[0], dtype=jnp.int32)[None, :]
    ).astype(jnp.float32)
    scale_src = jnp.sum(group_hits * deltas[None, :], axis=1)
    ends = [sum(CHUNKS[: c + 1]) for c in range(len(CHUNKS))]
    assert ends[-1] == source_count
    spans = [slice(end - size, end) for end, size in zip(ends, CHUNKS)]

    incidents = [incident[:, span] for span in spans]
    sent = list(incidents)
    sent[0] = jnp.concatenate([sent[0], split_gains(reflectivity)], axis=1)
    came = [send(x, "box", flip0) for x in sent]
    across_gains = join_gains(came[0][:, CHUNKS[0] :])
    across_incidents = [x[:, :size] for x, size in zip(came, CHUNKS)]

    tag = jnp.pad(onehot[:, None, :], ((0, 0), (0, 7), (0, width - box_count)))
    parts = [w[2, :, k] for w in (w_self, w_cross) for k in range(2)]
    parts = [send(pick(parts, quarter), "box", flip2)]
    parts += [send(parts[0], "src", k) for k in (1, 2, 3)]
    far_traces = send(jnp.concatenate([observed, tag], axis=1), "box", flip2)
    far_observed = far_traces[:, :source_count]
    far_onehot = far_traces[:, source_count, :box_count]
    parts = [pick(parts, quarter ^ k) for k in range(4)]
    far_self2, far_cross2 = join_parts(*parts[:2]), join_parts(*parts[2:])

    self0, cross0 = block_form(w_self[0]), block_form(w_cross[0])
    fields = [
        stage(scaled(x, reflectivity), scaled(p, across_gains), self0, cross0)
        for x, p in zip(incidents, across_incidents)
    ]
    nears = [send(x, "box", flip1) for x in fields]
    weights_self, weights_cross, _ = lax.optimization_barrier((w_self[1], w_cross[1], fields[0]))
    self1, cross1 = block_form(weights_self), block_form(weights_cross)
    fields = [stage(x, p, self1, cross1) for x, p in zip(fields, nears)]
    across_incidents, far_observed, _ = lax.optimization_barrier(
        (across_incidents, [far_observed[:, span] for span in spans], fields[0])
    )
    partners = [send(x, "box", flip2) for x in fields]
    weights_self, weights_cross, _ = lax.optimization_barrier((w_self[2], w_cross[2], fields[0]))
    self2, cross2 = block_form(weights_self), block_form(weights_cross)

    adjoints = []
    received = []
    for c, (span, field, partner) in enumerate(zip(spans, fields, partners)):
        if c:
            partner, _ = lax.optimization_barrier((partner, outgoing))
        top = stage(field, partner, self2, cross2)
        far_top = stage(partner, field, far_self2, far_cross2)
        own = trace_adjoint(top, onehot, observed[:, span], scale_src[span])
        far = trace_adjoint(far_top, far_onehot, far_observed[c], scale_src[span])
        adjoint = adjoint_apply(own, self2) + adjoint_apply(far, far_cross2)
        adjoints.append(adjoint.astype(jnp.bfloat16))
        outgoing = adjoint_apply(adjoints[-1], cross1).astype(jnp.bfloat16)
        received.append(send(outgoing, "box", flip1))
    adjoints = [
        (adjoint_apply(x, self1) + r.astype(jnp.float32)).astype(jnp.bfloat16)
        for x, r in zip(adjoints, received)
    ]
    own = across = 0.0
    for x, p, a in zip(incidents, across_incidents, adjoints):
        own += image_terms(x, adjoint_apply(a, self0))
        across += image_terms(p, adjoint_apply(a, cross0))

    share = node_count // src_devices
    upper = (box_index & flip0) != 0
    both = jnp.where(upper, jnp.stack([across, own]), jnp.stack([own, across]))
    pieces = both.reshape(2, box_count, src_devices, share).transpose(0, 2, 1, 3)
    pieces = pieces.reshape(2 * src_devices, box_count, share)
    groups = [
        [b * src_devices + s for b in (g, g + flip0) for s in range(src_devices)]
        for g in range(flip0)
    ]
    gathered = lax.all_to_all(pieces, ("box", "src"), 0, 0, axis_index_groups=groups)
    return jnp.sum(gathered, axis=0)


def solution(mesh):
    in_specs = (
        P("box", "src", None),
        P("box", None),
        P(None, "box", None, None, None),
        P(None, "box", None, None, None),
        P("box"),
        P("box", "src", None),
        P("src"),
        P(),
    )
    out_specs = P("box", "src")

    return jax.shard_map(body, mesh=mesh, in_specs=in_specs, out_specs=out_specs, check_vma=False)
```

```python
import jax
import jax.numpy as jnp
from jax import lax
from jax.sharding import PartitionSpec as P


CHUNKS = (64, 64)


def send(x, axis, flip):
    return lax.ppermute(x, axis, [(i, i ^ flip) for i in range(lax.axis_size(axis))])


def join_parts(real_part, imag_part):
    upper_rows = jnp.concatenate([real_part, imag_part], axis=2)
    lower_rows = jnp.concatenate([-imag_part, real_part], axis=2)
    return jnp.concatenate([upper_rows, lower_rows], axis=1)


def block_form(weights):
    return join_parts(weights[:, 0], weights[:, 1])


def forward_apply(values, block):
    return jnp.einsum("bsi,bij->bsj", values, block, preferred_element_type=jnp.float32)


def adjoint_apply(values, block):
    return jnp.einsum("bsj,bij->bsi", values, block, preferred_element_type=jnp.float32)


def stage(field, partner, own, cross):
    kept = forward_apply(field, own)
    return (kept + forward_apply(partner, cross)).astype(jnp.bfloat16)


def image_terms(incident, adjoint):
    products = incident.astype(jnp.float32) * adjoint
    node_count = products.shape[2] // 2
    return jnp.sum(products[..., :node_count] + products[..., node_count:], axis=1)


def scaled(field, gains):
    doubled = jnp.concatenate([gains, gains], axis=1)
    return (doubled[:, None, :] * field.astype(jnp.float32)).astype(jnp.bfloat16)


def split_gains(gains):
    high = lax.reduce_precision(gains, 8, 7)
    rest = gains - high
    middle = lax.reduce_precision(rest, 8, 7)
    low = rest - middle
    rows = jnp.stack(
        [
            jnp.concatenate([high, middle], axis=1),
            jnp.concatenate([low, jnp.zeros_like(low)], axis=1),
        ],
        axis=1,
    ).astype(jnp.bfloat16)
    return jnp.pad(rows, ((0, 0), (0, 6), (0, 0)))


def join_gains(rows):
    node_count = rows.shape[2] // 2
    rows = rows.astype(jnp.float32)
    return (rows[:, 0, :node_count] + rows[:, 0, node_count:]) + rows[:, 1, :node_count]


def trace_adjoint(field, onehot, observed, scale):
    predicted = jnp.einsum("kb,bsi->ksi", onehot, field, preferred_element_type=jnp.float32)
    residual = predicted - observed.astype(jnp.float32)
    node_count = residual.shape[2] // 2
    magnitude = residual[..., :node_count] ** 2 + residual[..., node_count:] ** 2
    damping = 1.0 / jnp.sqrt(1.0 + magnitude / scale[None, :, None] ** 2)
    adj_traces = (residual * jnp.concatenate([damping, damping], axis=2)).astype(jnp.bfloat16)
    return jnp.einsum("kb,ksi->bsi", onehot, adj_traces, preferred_element_type=jnp.float32).astype(
        jnp.bfloat16
    )


def pick(parts, index):
    low, high = (index & 1) != 0, (index & 2) != 0
    return jnp.where(high, jnp.where(low, parts[3], parts[2]), jnp.where(low, parts[1], parts[0]))


def body(incident, reflectivity, w_self, w_cross, receivers, observed, group_of, deltas):
    box_count, source_count, width = incident.shape
    node_count = width // 2
    box_devices = lax.axis_size("box")
    src_devices = lax.axis_size("src")
    flip0, flip1, flip2 = box_devices // 2, box_devices // 4, box_devices // 8
    box_index = lax.axis_index("box")
    quarter = lax.axis_index("src") % 4
    onehot = (
        (receivers - box_index * box_count)[:, None]
        == jnp.arange(box_count, dtype=jnp.int32)[None, :]
    ).astype(jnp.bfloat16)
    group_hits = (
        group_of[:, None] == jnp.arange(deltas.shape[0], dtype=jnp.int32)[None, :]
    ).astype(jnp.float32)
    scale_src = jnp.sum(group_hits * deltas[None, :], axis=1)
    ends = [sum(CHUNKS[: c + 1]) for c in range(len(CHUNKS))]
    assert ends[-1] == source_count
    spans = [slice(end - size, end) for end, size in zip(ends, CHUNKS)]

    incidents = [incident[:, spans[0]]]
    sent = [jnp.concatenate([incidents[0], split_gains(reflectivity)], axis=1)]
    for span in spans[1:]:
        later, _ = lax.optimization_barrier((incident, sent[-1]))
        incidents.append(later[:, span])
        sent.append(incidents[-1])
    came = [send(x, "box", flip0) for x in sent]
    across_gains = join_gains(came[0][:, CHUNKS[0] :])
    across_incidents = [x[:, :size] for x, size in zip(came, CHUNKS)]

    tag = jnp.pad(onehot[:, None, :], ((0, 0), (0, 7), (0, width - box_count)))
    parts = [w[2, :, k] for w in (w_self, w_cross) for k in range(2)]
    parts = [send(pick(parts, quarter), "box", flip2)]
    parts += [send(parts[0], "src", k) for k in (1, 2, 3)]
    far_traces = send(jnp.concatenate([observed, tag], axis=1), "box", flip2)
    far_observed = far_traces[:, :source_count]
    far_onehot = far_traces[:, source_count, :box_count]
    parts = [pick(parts, quarter ^ k) for k in range(4)]
    far_self2, far_cross2 = join_parts(*parts[:2]), join_parts(*parts[2:])

    self0, cross0 = block_form(w_self[0]), block_form(w_cross[0])
    fields = [
        stage(scaled(x, reflectivity), scaled(p, across_gains), self0, cross0)
        for x, p in zip(incidents, across_incidents)
    ]
    nears = [send(x, "box", flip1) for x in fields]
    weights_self, weights_cross, _ = lax.optimization_barrier((w_self[1], w_cross[1], fields[0]))
    self1, cross1 = block_form(weights_self), block_form(weights_cross)
    fields = [stage(x, p, self1, cross1) for x, p in zip(fields, nears)]
    across_incidents, far_observed, _ = lax.optimization_barrier(
        (across_incidents, [far_observed[:, span] for span in spans], fields[0])
    )
    partners = [send(x, "box", flip2) for x in fields]
    weights_self, weights_cross, _ = lax.optimization_barrier((w_self[2], w_cross[2], fields[0]))
    self2, cross2 = block_form(weights_self), block_form(weights_cross)

    adjoints = []
    received = []
    for c, (span, field, partner) in enumerate(zip(spans, fields, partners)):
        if c:
            partner, _ = lax.optimization_barrier((partner, outgoing))
        top = stage(field, partner, self2, cross2)
        far_top = stage(partner, field, far_self2, far_cross2)
        own = trace_adjoint(top, onehot, observed[:, span], scale_src[span])
        far = trace_adjoint(far_top, far_onehot, far_observed[c], scale_src[span])
        adjoint = adjoint_apply(own, self2) + adjoint_apply(far, far_cross2)
        adjoints.append(adjoint.astype(jnp.bfloat16))
        outgoing = adjoint_apply(adjoints[-1], cross1).astype(jnp.bfloat16)
        received.append(send(outgoing, "box", flip1))
    adjoints = [
        (adjoint_apply(x, self1) + r.astype(jnp.float32)).astype(jnp.bfloat16)
        for x, r in zip(adjoints, received)
    ]
    own = across = 0.0
    for x, p, a in zip(incidents, across_incidents, adjoints):
        own += image_terms(x, adjoint_apply(a, self0))
        across += image_terms(p, adjoint_apply(a, cross0))

    share = node_count // src_devices
    upper = (box_index & flip0) != 0
    both = jnp.where(upper, jnp.stack([across, own]), jnp.stack([own, across]))
    pieces = both.reshape(2, box_count, src_devices, share).transpose(0, 2, 1, 3)
    pieces = pieces.reshape(2 * src_devices, box_count, share)
    groups = [
        [b * src_devices + s for b in (g, g + flip0) for s in range(src_devices)]
        for g in range(flip0)
    ]
    gathered = lax.all_to_all(pieces, ("box", "src"), 0, 0, axis_index_groups=groups)
    return jnp.sum(gathered, axis=0)


def solution(mesh):
    in_specs = (
        P("box", "src", None),
        P("box", None),
        P(None, "box", None, None, None),
        P(None, "box", None, None, None),
        P("box"),
        P("box", "src", None),
        P("src"),
        P(),
    )
    out_specs = P("box", "src")

    return jax.shard_map(body, mesh=mesh, in_specs=in_specs, out_specs=out_specs, check_vma=False)
```
